1024 devices in a mesh: tower: 32 (over x, y_lo), intra: 32 (over y_hi, z, core).
Axes of the slice: x: 8, y: 8 (y_hi: 2, y_lo: 4; y = y_hi * 4 + y_lo), z: 8, core: 2. Of those that a mesh axis runs over, the one named last changes fastest.
Arguments:
- embeddings: bfloat16 [8192, 131072], P(None, ('tower', 'intra')), may hold values from -6 to 6
- feature_assign: int32 [32, 32], P('tower'), may hold values from 0 to 31, each once within a row
- sample_owner: int32 [8192], replicated, may hold values from 0 to 8191, each once
- first_weight: bfloat16 [64, 2048, 1024], P('tower'), may hold values from -0.125 to 0.125
- first_bias: float32 [64, 1024], P('tower'), may hold values from -3 to 3
- tower_weight: bfloat16 [64, 1024, 256], P('tower'), may hold values from -0.1875 to 0.1875
- tower_bias: float32 [64, 256], P('tower'), may hold values from -3 to 3
- proj_weight: bfloat16 [128, 128], replicated, may hold values from -0.5 to 0.5
Outputs:
- interaction: bfloat16 [8192, 128, 128], P(('tower', 'intra'))
The draws below stay inside these ranges and needn't reach their ends.
Inputs may be any that keep to these rules, and one draw needn't show every extreme that they name: `feature_assign`: each row is a permutation of 0 to 31. `sample_owner`: a permutation of 0 to 8191.
All inputs are finite; a program needn't handle non-finite values.
Results may differ from the reference program's by a relative error of at most 0.0034.
Values may be sent and summed in bfloat16 or wider, within the bound.
A program may use at most 64 MiB of HBM per device.

```python
import jax
import jax.numpy as jnp
from jax import lax

EDIM = 128
TFEAT = 16
HID = 1024
TOUT = 256
TOW_DEV = 2
SD = 8
TIN = 2048
TVEC = 2
FPT = 32
TOWERS = 64
NVEC = 128
FEATURES = 1024
SAMPLES = 8192
N_TOWER = 32
N_INTRA = 32


def shard_levels(own_key, shape, shards, smallest, high):
    factor_of, own = 1.0, jax.random.fold_in(own_key, 6)
    for dim, parts in shards:
        draws = jnp.exp(jax.random.uniform(jax.random.fold_in(own, dim), (parts,), jnp.float32, smallest / len(shards), high / len(shards)))
        factor_of = factor_of * jnp.repeat(draws, shape[dim] // parts).reshape([-1 if axis == dim else 1 for axis in range(len(shape))])
    return factor_of


def scatter_about(rng, shape, deviation, bound, cuts=(), kind=jnp.bfloat16):
    level = shard_levels(rng, shape, cuts, -0.22, 0.18) if cuts else 1.0
    values = jax.random.normal(rng, shape, jnp.float32) * deviation * level
    return jnp.minimum(jnp.maximum(values, -bound), bound).astype(kind)


def setup_inputs(seed: int = 0) -> dict:
    arg_keys = jax.random.split(jax.random.key(seed), 9)
    return {
        "embeddings": scatter_about(arg_keys[0], (SAMPLES, FEATURES * EDIM), 1.0, 6.0, ((1, 1024),)),
        "feature_assign": jax.vmap(lambda own: jax.random.permutation(own, FPT))(jax.random.split(arg_keys[1], N_TOWER)).reshape((N_TOWER, FPT)).astype(jnp.int32),
        "sample_owner": jax.random.permutation(arg_keys[2], SAMPLES).astype(jnp.int32),
        "first_weight": scatter_about(arg_keys[3], (TOWERS, TIN, HID), TIN ** -0.5, 0.125, ((0, 32),)),
        "first_bias": scatter_about(arg_keys[4], (TOWERS, HID), 0.5, 3.0, ((0, 32),), jnp.float32),
        "tower_weight": scatter_about(arg_keys[5], (TOWERS, HID, TOUT), HID ** -0.5, 0.1875, ((0, 32),)),
        "tower_bias": scatter_about(arg_keys[6], (TOWERS, TOUT), 0.5, 3.0, ((0, 32),), jnp.float32),
        "proj_weight": scatter_about(arg_keys[7], (NVEC, EDIM), NVEC ** -0.5, 0.5),
    }


def reference(embeddings, feature_assign, sample_owner, first_weight, first_bias, tower_weight, tower_bias, proj_weight):
    ordered = jnp.take(embeddings, sample_owner, axis=0)
    tower_ids = jnp.arange(TOWERS, dtype=jnp.int32)

    def one_tower(tower_number):
        tower_index = tower_number // TOW_DEV
        slot_index = tower_number % TOW_DEV
        assign_row = feature_assign[tower_index]
        selected = lax.dynamic_slice_in_dim(assign_row, (slot_index * TFEAT).astype(jnp.int32), TFEAT)
        feature_ids = (tower_index * FPT + selected).astype(jnp.int32)
        columns = (feature_ids[:, None] * EDIM + jnp.arange(EDIM, dtype=jnp.int32)[None, :]).reshape(-1)
        inputs = jnp.take(ordered, columns, axis=1).astype(jnp.float32)
        hidden = jnp.dot(inputs, first_weight[tower_number].astype(jnp.float32), precision=lax.Precision.HIGHEST)
        hidden = jnp.maximum(hidden + first_bias[tower_number], 0.0).astype(jnp.bfloat16)
        result = jnp.dot(hidden.astype(jnp.float32), tower_weight[tower_number].astype(jnp.float32), precision=lax.Precision.HIGHEST)
        result = result + tower_bias[tower_number]
        return jnp.maximum(result, 0.0).astype(jnp.bfloat16)

    tower_outputs = lax.map(one_tower, tower_ids)
    vectors = tower_outputs.reshape(TOWERS, SAMPLES, TVEC, EDIM).transpose(1, 0, 2, 3).reshape(SAMPLES, NVEC, EDIM)
    block = SD * N_INTRA
    blocks = vectors.reshape(SAMPLES // block, block, NVEC, EDIM)
    weight_wide = proj_weight.astype(jnp.float32)

    def interact(vector_block):
        vector_wide = vector_block.astype(jnp.float32)
        gram_matrix = jnp.einsum("pie,pje->pij", vector_wide, vector_wide, precision=lax.Precision.HIGHEST) / EDIM
        result = jnp.einsum("pij,je->pie", gram_matrix, weight_wide, precision=lax.Precision.HIGHEST)
        return result.astype(jnp.bfloat16)

    return lax.map(interact, blocks).reshape(SAMPLES, NVEC, EDIM)
```

```python
import functools

import jax
import jax.numpy as jnp
from jax import lax
from jax.experimental import pallas as pl
from jax.experimental.pallas import tpu as pltpu
from jax.sharding import PartitionSpec as P

EDIM = 128
TOW_DEV = 2
TFEAT = 16
TIN = 2048
HID = 1024
TOUT = 256
SD = 8
QV = 4
N_TOWER = 32
N_INTRA = 32
SAMPLES = 8192
CHUNKS = ((4, 5), (3, 6), (2, 7), (1, 0))
NCH = len(CHUNKS)
POS = 8
ROWS = POS * SD
EMB_PARTS = 4
MESH = pl.DeviceIdType.MESH
BF16 = jnp.bfloat16
F32 = jnp.float32


def kernel(
    owner, assign, emb_hbm, w1_hbm, b1, w2_hbm, b2, proj, out,
    emb_b, emb_f, stage, r0, r1, r2, r3, w1, w2, rows_f, x, hid, send, own, own_f, out_f, proj_f,
    emb_sem, w_sem, send_sem, recv_sem, send2_sem, recv2_sem,
):
    recv = (r0, r1, r2, r3)
    tower = lax.axis_index("tower")
    me = lax.axis_index("intra")
    tx, ty = tower // 4, tower % 4
    y_hi, z, core = me // 16, (me // 2) % 8, me % 2

    part = SAMPLES // EMB_PARTS
    emb_copies = [
        pltpu.make_async_copy(
            emb_hbm.at[pl.ds(i * part, part)], emb_b.at[pl.ds(i * part, part)], emb_sem.at[i]
        )
        for i in range(EMB_PARTS)
    ]
    for copy in emb_copies:
        copy.start()

    barrier = pltpu.get_barrier_semaphore()

    @pl.loop(1, N_INTRA)
    def _(k):
        pl.semaphore_signal(
            barrier, inc=1, device_id={"intra": lax.rem(me + k, N_INTRA)}, device_id_type=MESH
        )
        pl.semaphore_signal(
            barrier, inc=1, device_id={"tower": lax.rem(tower + k, N_TOWER)}, device_id_type=MESH
        )

    for i, copy in enumerate(emb_copies):
        copy.wait()
        emb_f[pl.ds(i * part, part), :] = emb_b[pl.ds(i * part, part), :].astype(F32)

    w_copies = [
        pltpu.make_async_copy(w1_hbm, w1, w_sem.at[0]),
        pltpu.make_async_copy(w2_hbm, w2, w_sem.at[1]),
    ]
    for copy in w_copies:
        copy.start()

    def towers_of(c):
        return [
            ((tx + dx) % 8) * 4 + (ty + dy) % 4 for dx in CHUNKS[c] for dy in range(4)
        ]

    def peer_of(k):
        kk = 7 - k % 8
        odd = kk % 2
        dz = odd * ((kk + 1) // 2) + (1 - odd) * (8 - kk // 2)
        dy = 1 - (k // 8) % 2
        dc = 1 - k // 16
        return ((y_hi + dy) % 2) * 16 + ((z + dz) % 8) * 2 + (core + dc) % 2

    def gather(targets, peer):
        for pos in range(POS):
            base = (targets[pos] * N_INTRA + peer) * SD
            for r in range(SD):
                rows_f[pl.ds(pos * SD + r, 1), :] = emb_f[pl.ds(owner[base + r], 1), :]
        return rows_f[...].astype(BF16)

    pl.semaphore_wait(barrier, (N_INTRA - 1) + (N_TOWER - 1))

    for c in range(NCH):
        targets = towers_of(c)

        def copy_of(k, c=c):
            return pltpu.make_async_remote_copy(
                src_ref=stage.at[c, k],
                dst_ref=recv[c].at[me],
                send_sem=send_sem.at[c],
                recv_sem=recv_sem.at[c],
                device_id={"intra": peer_of(k)},
                device_id_type=MESH,
            )

        @pl.loop(0, N_INTRA - 1)
        def _(k, c=c, targets=targets, copy_of=copy_of):
            stage[c, k] = gather(targets, peer_of(k))

            @pl.when(k > 0)
            def _():
                copy_of(k - 1).start()

        recv[c][me] = gather(targets, me)
        copy_of(N_INTRA - 2).start()

    for copy in w_copies:
        copy.wait()

    for c in range(NCH):
        targets = towers_of(c)
        arrived = recv[c].at[pl.ds(0, N_INTRA - 1)]
        pltpu.make_async_copy(arrived, arrived, recv_sem.at[c]).wait()
        for m in range(TOW_DEV):
            for s in range(TFEAT):
                x[m, :, s * EDIM : (s + 1) * EDIM] = recv[c][assign[0, m * TFEAT + s]]
        result = []
        for m in range(TOW_DEV):
            for n in range(HID // 256):
                cols = slice(n * 256, (n + 1) * 256)
                total = jnp.dot(x[m], w1[m, :, cols], preferred_element_type=F32)
                hid[m, :, cols] = jnp.maximum(total + b1[pl.ds(m, 1), cols], 0.0).astype(BF16)
            total = jnp.dot(hid[m], w2[m], preferred_element_type=F32)
            result.append(jnp.maximum(total + b2[pl.ds(m, 1), :], 0.0))
        for pos in range(POS):
            rows = slice(pos * SD, (pos + 1) * SD)
            block = jnp.concatenate(
                [result[q // 2][rows, (q % 2) * EDIM : (q % 2 + 1) * EDIM] for q in range(QV)], axis=0
            )
            if CHUNKS[c][pos // 4] == 0 and pos % 4 == 0:
                own[tower] = block.astype(BF16)
            else:
                send[c, pos] = block.astype(BF16)
        for pos in range(POS):
            if CHUNKS[c][pos // 4] == 0 and pos % 4 == 0:
                continue
            pltpu.make_async_remote_copy(
                src_ref=send.at[c, pos],
                dst_ref=own.at[tower],
                send_sem=send2_sem,
                recv_sem=recv2_sem,
                device_id={"tower": targets[pos]},
                device_id_type=MESH,
            ).start()

    proj_f[...] = proj[...].astype(F32)
    weight = jnp.concatenate([proj_f[pl.ds(q, N_TOWER, stride=QV), :] for q in range(QV)], axis=0)
    weight = weight.astype(BF16)

    arrived = own.at[pl.ds(0, N_TOWER - 1)]
    pltpu.make_async_copy(arrived, arrived, recv2_sem).wait()

    own_f[...] = own[...].astype(F32).reshape(N_TOWER * QV * SD, EDIM)
    for r in range(SD):
        vectors = jnp.concatenate(
            [own_f[pl.ds(q * SD + r, N_TOWER, stride=QV * SD), :] for q in range(QV)], axis=0
        ).astype(BF16)
        gram = lax.dot_general(
            vectors, vectors, (((1,), (1,)), ((), ())), preferred_element_type=F32
        ) * (1.0 / EDIM)
        high = gram.astype(BF16)
        low = (gram - high.astype(F32)).astype(BF16)
        result = jnp.dot(high, weight, preferred_element_type=F32)
        result = result + jnp.dot(low, weight, preferred_element_type=F32)
        for q in range(QV):
            out_f[r, pl.ds(q, N_TOWER, stride=QV), :] = result[q * N_TOWER : (q + 1) * N_TOWER, :]
        out[r] = out_f[r].astype(BF16)

    for c in range(NCH):
        left = stage.at[c, pl.ds(0, N_INTRA - 1)]
        pltpu.make_async_copy(left, left, send_sem.at[c]).wait()
    left = own.at[pl.ds(0, N_TOWER - 1)]
    pltpu.make_async_copy(left, left, send2_sem).wait()


def shards(
    embeddings,
    feature_assign,
    sample_owner,
    first_weight,
    first_bias,
    tower_weight,
    tower_bias,
    proj_weight,
):
    vmem = pl.BlockSpec(memory_space=pltpu.VMEM)
    smem = pl.BlockSpec(memory_space=pltpu.SMEM)
    hbm = pl.BlockSpec(memory_space=pl.ANY)
    dma = pltpu.SemaphoreType.DMA
    recv = [pltpu.VMEM((N_INTRA, ROWS, EDIM), BF16) for _ in range(NCH)]
    return pl.pallas_call(
        kernel,
        out_shape=jax.ShapeDtypeStruct((SD, N_TOWER * QV, EDIM), BF16),
        in_specs=[smem, smem, hbm, hbm, vmem, hbm, vmem, vmem],
        out_specs=vmem,
        scratch_shapes=[
            pltpu.VMEM((SAMPLES, EDIM), BF16),
            pltpu.VMEM((SAMPLES, EDIM), F32),
            pltpu.VMEM((NCH, N_INTRA, ROWS, EDIM), BF16),
            *recv,
            pltpu.VMEM((TOW_DEV, TIN, HID), BF16),
            pltpu.VMEM((TOW_DEV, HID, TOUT), BF16),
            pltpu.VMEM((ROWS, EDIM), F32),
            pltpu.VMEM((TOW_DEV, ROWS, TIN), BF16),
            pltpu.VMEM((TOW_DEV, ROWS, HID), BF16),
            pltpu.VMEM((NCH, POS, QV * SD, EDIM), BF16),
            pltpu.VMEM((N_TOWER, QV * SD, EDIM), BF16),
            pltpu.VMEM((N_TOWER * QV * SD, EDIM), F32),
            pltpu.VMEM((SD, N_TOWER * QV, EDIM), F32),
            pltpu.VMEM((N_TOWER * QV, EDIM), F32),
            dma((EMB_PARTS,)),
            dma((2,)),
            dma((NCH,)),
            dma((NCH,)),
            dma,
            dma,
        ],
        compiler_params=pltpu.CompilerParams(
            collective_id=0, has_side_effects=True, vmem_limit_bytes=48 * 1024 * 1024
        ),
        name="towers",
    )(
        sample_owner,
        feature_assign,
        embeddings,
        first_weight,
        first_bias,
        tower_weight,
        tower_bias,
        proj_weight,
    )


def solution(mesh):
    return jax.shard_map(
        shards,
        mesh=mesh,
        in_specs=(
            P(None, ("tower", "intra")),
            P("tower", None),
            P(),
            P("tower", None, None),
            P("tower", None),
            P("tower", None, None),
            P("tower", None),
            P(),
        ),
        out_specs=P(("tower", "intra"), None, None),
        check_vma=False,
    )
```

```python
import jax
import jax.numpy as jnp
from jax import lax
from jax.experimental import pallas as pl
from jax.experimental.pallas import tpu as pltpu
from jax.sharding import PartitionSpec as P

EDIM = 128
TOW_DEV = 2
TFEAT = 16
TIN = 2048
HID = 1024
TOUT = 256
SD = 8
QV = 4
N_TOWER = 32
N_INTRA = 32
SAMPLES = 8192
CHUNKS = ((4, 5), (3, 6), (2, 7), (1,), (0,))
NCH = len(CHUNKS)
RUN = 4
ROWS = tuple(len(offsets) * RUN * SD for offsets in CHUNKS)
FIRST = tuple(RUN * sum(len(offsets) for offsets in CHUNKS[:c]) for c in range(NCH))
EMB_PARTS = 4
AHEAD = 16
MESH = pl.DeviceIdType.MESH
BF16 = jnp.bfloat16
F32 = jnp.float32


def kernel(
    owner_hbm, assign_hbm, emb_hbm, w1_hbm, b1_hbm, w2_hbm, b2_hbm, proj_hbm, out, *scratch
):
    stage, recv = scratch[:NCH], scratch[NCH : 2 * NCH]
    (
        owner, assign, b1, b2, proj, emb_b, emb_f, w1, w2, rows_f, x, hid, send, own, own_f, out_f, proj_f,
        emb_sem, table_sem, w_sem, send_sem, recv_sem, send2_sem, recv2_sem,
    ) = scratch[2 * NCH :]
    tower = lax.axis_index("tower")
    me = lax.axis_index("intra")
    tx = tower // RUN
    y = (me // 16) * RUN + tower % RUN
    z, core = (me // 2) % 8, me % 2

    part = SAMPLES // EMB_PARTS
    emb_copies = [
        pltpu.make_async_copy(
            emb_hbm.at[pl.ds(i * part, part)], emb_b.at[pl.ds(i * part, part)], emb_sem.at[i]
        )
        for i in range(EMB_PARTS)
    ]
    owner_copy = pltpu.make_async_copy(owner_hbm, owner, table_sem)
    others = ((assign_hbm, assign), (b1_hbm, b1), (b2_hbm, b2), (proj_hbm, proj), (w2_hbm, w2), (w1_hbm, w1))
    w_copies = [
        pltpu.make_async_copy(source, target, w_sem.at[i]) for i, (source, target) in enumerate(others)
    ]
    owner_copy.start()
    for copy in emb_copies:
        copy.start()

    barrier = pltpu.get_barrier_semaphore()

    def place(px, py, pz, pcore):
        return {"tower": px * RUN + py % RUN, "intra": (py // RUN) * 16 + pz * 2 + pcore}

    def y_step(dx, step):
        return (step % 2) * (2 - step) + (step // 2) * (1 - step % 2) * (2 - 4 * (dx % 2))

    @pl.loop(1, N_INTRA)
    def _(k):
        pl.semaphore_signal(
            barrier, inc=1, device_id={"intra": lax.rem(me + k, N_INTRA)}, device_id_type=MESH
        )
        dx = k // RUN
        sender = place((tx + 8 - dx) % 8, (y + 8 - y_step(dx, k % RUN)) % 8, z, core)
        pl.semaphore_signal(barrier, inc=1, device_id=sender, device_id_type=MESH)

    for i, copy in enumerate(emb_copies):
        copy.wait()
        emb_f[pl.ds(i * part, part), :] = emb_b[pl.ds(i * part, part), :].astype(F32)
    for copy in w_copies:
        copy.start()
    owner_copy.wait()

    def steps_of(c):
        return [(dx, y_step(dx, step)) for dx in CHUNKS[c] for step in range(RUN)]

    def peer_of(k):
        kk = 7 - k % 8
        odd = kk % 2
        dz = odd * ((kk + 1) // 2) + (1 - odd) * (8 - kk // 2)
        dy = 1 - (k // 8) % 2
        dc = 1 - k // 16
        return tx, (y + RUN * dy) % 8, (z + dz) % 8, (core + dc) % 2

    def gather(steps, peer):
        rows = len(steps) * SD
        px, py, pz, pcore = peer
        for pos, (dx, dy) in enumerate(steps):
            target = place((px + dx) % 8, (py + 8 + dy) % 8, pz, pcore)
            base = (target["tower"] * N_INTRA + target["intra"]) * SD
            for r in range(SD):
                rows_f[pl.ds(pos * SD + r, 1), :] = emb_f[pl.ds(owner[base + r], 1), :]
        return rows_f[pl.ds(0, rows), :].astype(BF16)

    for c in range(NCH):
        steps = steps_of(c)

        def copy_of(k, c=c):
            return pltpu.make_async_remote_copy(
                src_ref=stage[c].at[k],
                dst_ref=recv[c].at[me],
                send_sem=send_sem.at[c],
                recv_sem=recv_sem.at[c],
                device_id=place(*peer_of(k)),
                device_id_type=MESH,
            )

        if c == 0:

            @pl.loop(0, AHEAD)
            def _(k, steps=steps):
                stage[0][k] = gather(steps, peer_of(k))

            pl.semaphore_wait(barrier, (N_INTRA - 1) + (N_TOWER - 1))

            @pl.loop(0, AHEAD - 1)
            def _(k, copy_of=copy_of):
                copy_of(k).start()

        begin = AHEAD if c == 0 else 0

        @pl.loop(begin, N_INTRA - 1)
        def _(k, c=c, steps=steps, copy_of=copy_of):
            stage[c][k] = gather(steps, peer_of(k))

            @pl.when(k > 0)
            def _():
                copy_of(k - 1).start()

        recv[c][me] = gather(steps, (tx, y, z, core))
        copy_of(N_INTRA - 2).start()

    for copy in w_copies:
        copy.wait()

    proj_f[...] = proj[...].astype(F32)
    weight = jnp.concatenate([proj_f[pl.ds(q, N_TOWER, stride=QV), :] for q in range(QV)], axis=0)
    proj[...] = weight.astype(BF16)

    for c in range(NCH):
        steps = steps_of(c)
        rows = ROWS[c]
        arrived = recv[c].at[pl.ds(0, N_INTRA - 1)]
        pltpu.make_async_copy(arrived, arrived, recv_sem.at[c]).wait()
        for m in range(TOW_DEV):
            for s in range(TFEAT):
                x[m, 0:rows, s * EDIM : (s + 1) * EDIM] = recv[c][assign[0, m * TFEAT + s]]
        result = []
        for m in range(TOW_DEV):
            for n in range(HID // 256):
                cols = slice(n * 256, (n + 1) * 256)
                total = jnp.dot(x[m, 0:rows, :], w1[m, :, cols], preferred_element_type=F32)
                hid[m, 0:rows, cols] = jnp.maximum(total + b1[pl.ds(m, 1), cols], 0.0).astype(BF16)
            total = jnp.dot(hid[m, 0:rows, :], w2[m], preferred_element_type=F32)
            result.append(jnp.maximum(total + b2[pl.ds(m, 1), :], 0.0))
        copies = []
        for pos, (dx, dy) in enumerate(steps):
            block = jnp.concatenate(
                [
                    result[q // 2][pos * SD : (pos + 1) * SD, (q % 2) * EDIM : (q % 2 + 1) * EDIM]
                    for q in range(QV)
                ],
                axis=0,
            ).astype(BF16)
            if (dx, dy) == (0, 0):
                own[tower] = block
                continue
            slot = FIRST[c] + pos
            send[slot] = block
            copies.append(
                pltpu.make_async_remote_copy(
                    src_ref=send.at[slot],
                    dst_ref=own.at[tower],
                    send_sem=send2_sem,
                    recv_sem=recv2_sem,
                    device_id=place((tx + dx) % 8, (y + 8 + dy) % 8, z, core),
                    device_id_type=MESH,
                )
            )
        for copy in copies:
            copy.start()

    arrived = own.at[pl.ds(0, N_TOWER - 1)]
    pltpu.make_async_copy(arrived, arrived, recv2_sem).wait()

    own_f[...] = own[...].astype(F32).reshape(N_TOWER * QV * SD, EDIM)
    weight = proj[...]
    for r in range(SD):
        vectors = jnp.concatenate(
            [own_f[pl.ds(q * SD + r, N_TOWER, stride=QV * SD), :] for q in range(QV)], axis=0
        ).astype(BF16)
        gram = lax.dot_general(
            vectors, vectors, (((1,), (1,)), ((), ())), preferred_element_type=F32
        ) * (1.0 / EDIM)
        high = gram.astype(BF16)
        low = (gram - high.astype(F32)).astype(BF16)
        result = jnp.dot(high, weight, preferred_element_type=F32)
        result = result + jnp.dot(low, weight, preferred_element_type=F32)
        for q in range(QV):
            out_f[r, pl.ds(q, N_TOWER, stride=QV), :] = result[q * N_TOWER : (q + 1) * N_TOWER, :]
        out[r] = out_f[r].astype(BF16)

    for c in range(NCH):
        left = stage[c].at[pl.ds(0, N_INTRA - 1)]
        pltpu.make_async_copy(left, left, send_sem.at[c]).wait()
    left = own.at[pl.ds(0, N_TOWER - 1)]
    pltpu.make_async_copy(left, left, send2_sem).wait()


def shards(
    embeddings,
    feature_assign,
    sample_owner,
    first_weight,
    first_bias,
    tower_weight,
    tower_bias,
    proj_weight,
):
    vmem = pl.BlockSpec(memory_space=pltpu.VMEM)
    hbm = pl.BlockSpec(memory_space=pltpu.HBM)
    dma = pltpu.SemaphoreType.DMA
    blocks = [pltpu.VMEM((N_INTRA, rows, EDIM), BF16) for rows in ROWS]
    return pl.pallas_call(
        kernel,
        out_shape=jax.ShapeDtypeStruct((SD, N_TOWER * QV, EDIM), BF16),
        in_specs=[hbm] * 8,
        out_specs=vmem,
        scratch_shapes=[
            *blocks,
            *blocks,
            pltpu.SMEM((SAMPLES,), jnp.int32),
            pltpu.SMEM((1, TOW_DEV * TFEAT), jnp.int32),
            pltpu.VMEM((TOW_DEV, HID), F32),
            pltpu.VMEM((TOW_DEV, TOUT), F32),
            pltpu.VMEM((N_TOWER * QV, EDIM), BF16),
            pltpu.VMEM((SAMPLES, EDIM), BF16),
            pltpu.VMEM((SAMPLES, EDIM), F32),
            pltpu.VMEM((TOW_DEV, TIN, HID), BF16),
            pltpu.VMEM((TOW_DEV, HID, TOUT), BF16),
            pltpu.VMEM((max(ROWS), EDIM), F32),
            pltpu.VMEM((TOW_DEV, max(ROWS), TIN), BF16),
            pltpu.VMEM((TOW_DEV, max(ROWS), HID), BF16),
            pltpu.VMEM((N_TOWER, QV * SD, EDIM), BF16),
            pltpu.VMEM((N_TOWER, QV * SD, EDIM), BF16),
            pltpu.VMEM((N_TOWER * QV * SD, EDIM), F32),
            pltpu.VMEM((SD, N_TOWER * QV, EDIM), F32),
            pltpu.VMEM((N_TOWER * QV, EDIM), F32),
            dma((EMB_PARTS,)),
            dma,
            dma((6,)),
            dma((NCH,)),
            dma((NCH,)),
            dma,
            dma,
        ],
        compiler_params=pltpu.CompilerParams(
            collective_id=0, has_side_effects=True, vmem_limit_bytes=67043328
        ),
        name="towers",
    )(
        sample_owner,
        feature_assign,
        embeddings,
        first_weight,
        first_bias,
        tower_weight,
        tower_bias,
        proj_weight,
    )


def solution(mesh):
    return jax.shard_map(
        shards,
        mesh=mesh,
        in_specs=(
            P(None, ("tower", "intra")),
            P("tower", None),
            P(),
            P("tower", None, None),
            P("tower", None),
            P("tower", None, None),
            P("tower", None),
            P(),
        ),
        out_specs=P(("tower", "intra"), None, None),
        check_vma=False,
    )
```

```python
import jax
import jax.numpy as jnp
from jax import lax
from jax.experimental import pallas as pl
from jax.experimental.pallas import tpu as pltpu
from jax.sharding import PartitionSpec as P

EDIM = 128
TOW_DEV = 2
TFEAT = 16
TIN = 2048
HID = 1024
TOUT = 256
SD = 8
QV = 4
N_TOWER = 32
N_INTRA = 32
SAMPLES = 8192
CHUNKS = ((4, 5), (3, 6), (2, 7), (1,), (0,))
NCH = len(CHUNKS)
RUN = 4
ROWS = tuple(len(offsets) * RUN * SD for offsets in CHUNKS)
FIRST = tuple(RUN * sum(len(offsets) for offsets in CHUNKS[:c]) for c in range(NCH))
EMB_PARTS = 4
EAGER = 2
MESH = pl.DeviceIdType.MESH
BF16 = jnp.bfloat16
F32 = jnp.float32


def kernel(
    owner_hbm, assign_hbm, emb_hbm, w1_hbm, b1_hbm, w2_hbm, b2_hbm, proj_hbm, out, *scratch
):
    stage, recv = scratch[:NCH], scratch[NCH : 2 * NCH]
    (
        owner, assign, b1, b2, proj, emb_b, emb_f, w1, w2, rows_f, x, hid, send, own, own_f, out_f, proj_f,
        emb_sem, table_sem, w_sem, send_sem, recv_sem, send2_sem, recv2_sem, ready, ready2,
    ) = scratch[2 * NCH :]
    tower = lax.axis_index("tower")
    me = lax.axis_index("intra")
    tx = tower // RUN
    y = (me // 16) * RUN + tower % RUN
    z, core = (me // 2) % 8, me % 2

    part = SAMPLES // EMB_PARTS
    emb_copies = [
        pltpu.make_async_copy(
            emb_hbm.at[pl.ds(i * part, part)], emb_b.at[pl.ds(i * part, part)], emb_sem.at[i]
        )
        for i in range(EMB_PARTS)
    ]
    owner_copy = pltpu.make_async_copy(owner_hbm, owner, table_sem)
    others = ((assign_hbm, assign), (b1_hbm, b1), (b2_hbm, b2), (proj_hbm, proj), (w2_hbm, w2), (w1_hbm, w1))
    w_copies = [
        pltpu.make_async_copy(source, target, w_sem.at[i]) for i, (source, target) in enumerate(others)
    ]
    owner_copy.start()
    for copy in emb_copies:
        copy.start()

    barrier = pltpu.get_barrier_semaphore()

    def place(px, py, pz, pcore):
        return {"tower": px * RUN + py % RUN, "intra": (py // RUN) * 16 + pz * 2 + pcore}

    def y_step(dx, step):
        return (step % 2) * (2 - step) + (step // 2) * (1 - step % 2) * (2 - 4 * (dx % 2))

    def member(order):
        return tx, (y % RUN) + RUN * ((order // 2) % 2), order // 4, order % 2

    def source_of(k):
        dx = k // RUN
        return (tx + 8 - dx) % 8, (y + 8 - y_step(dx, k % RUN)) % 8

    def target_of(dx, dy):
        return (tx + dx) % 8, (y + 8 + dy) % 8

    order = z * 4 + (y // RUN) * 2 + core
    rank = y * 8 + tx

    @pl.loop(order + 1, N_INTRA)
    def _(later):
        pl.semaphore_signal(barrier, inc=1, device_id=place(*member(later)), device_id_type=MESH)

    def greet(k, count):
        sx, sy = source_of(k)
        gx, gy = target_of(k // RUN, y_step(k // RUN, k % RUN))

        @pl.when(sy * 8 + sx > rank)
        def _():
            pl.semaphore_signal(barrier, inc=1, device_id=place(sx, sy, z, core), device_id_type=MESH)

        @pl.when(gy * 8 + gx > rank)
        def _():
            pl.semaphore_signal(barrier, inc=1, device_id=place(gx, gy, z, core), device_id_type=MESH)

        count = count + jnp.where(sy * 8 + sx < rank, 1, 0)
        return count + jnp.where(gy * 8 + gx < rank, 1, 0)

    earlier = lax.fori_loop(1, N_TOWER, greet, order)

    for i, copy in enumerate(emb_copies):
        copy.wait()
        emb_f[pl.ds(i * part, part), :] = emb_b[pl.ds(i * part, part), :].astype(F32)
    for copy in w_copies:
        copy.start()
    owner_copy.wait()

    def steps_of(c):
        return [(dx, y_step(dx, step)) for dx in CHUNKS[c] for step in range(RUN)]

    def peer_of(k):
        kk = 7 - k % 8
        odd = kk % 2
        dz = odd * ((kk + 1) // 2) + (1 - odd) * (8 - kk // 2)
        dy = 1 - (k // 8) % 2
        dc = 1 - k // 16
        return tx, (y + RUN * dy) % 8, (z + dz) % 8, (core + dc) % 2

    def gather(steps, peer):
        rows = len(steps) * SD
        px, py, pz, pcore = peer
        for pos, (dx, dy) in enumerate(steps):
            target = place((px + dx) % 8, (py + 8 + dy) % 8, pz, pcore)
            base = (target["tower"] * N_INTRA + target["intra"]) * SD
            for r in range(SD):
                rows_f[pl.ds(pos * SD + r, 1), :] = emb_f[pl.ds(owner[base + r], 1), :]
        return rows_f[pl.ds(0, rows), :].astype(BF16)

    @pl.when(earlier > 0)
    def _():
        pl.semaphore_wait(barrier, earlier)

    @pl.loop(0, order)
    def _(sooner):
        pl.semaphore_signal(ready.at[me], inc=1, device_id=place(*member(sooner)), device_id_type=MESH)

    @pl.loop(1, N_TOWER)
    def _(k):
        sx, sy = source_of(k)

        @pl.when(sy * 8 + sx < rank)
        def _():
            pl.semaphore_signal(
                ready2.at[k], inc=1, device_id=place(sx, sy, z, core), device_id_type=MESH
            )

    def copy_of(c, slot, peer):
        return pltpu.make_async_remote_copy(
            src_ref=stage[c].at[slot],
            dst_ref=recv[c].at[me],
            send_sem=send_sem.at[c],
            recv_sem=recv_sem.at[c],
            device_id=place(*peer),
            device_id_type=MESH,
        )

    @pl.loop(0, N_INTRA)
    def _(k):
        level = k // 4
        down = jnp.where(level < z, 1, 0)
        at = (down * (z - 1 - level) + (1 - down) * level) * 4 + k % 4
        peer = member(at)

        @pl.when(at != order)
        def _():
            for c in range(EAGER):
                stage[c][k] = gather(steps_of(c), peer)

            @pl.when(at > order)
            def _():
                pl.semaphore_wait(ready.at[place(*peer)["intra"]], 1)

            for c in range(EAGER):
                copy_of(c, k, peer).start()

    for c in range(EAGER):
        recv[c][me] = gather(steps_of(c), (tx, y, z, core))

    for c in range(EAGER, NCH):
        steps = steps_of(c)

        @pl.loop(0, N_INTRA - 1)
        def _(k, c=c, steps=steps):
            stage[c][k] = gather(steps, peer_of(k))

            @pl.when(k > 0)
            def _():
                copy_of(c, k - 1, peer_of(k - 1)).start()

        recv[c][me] = gather(steps, (tx, y, z, core))
        copy_of(c, N_INTRA - 2, peer_of(N_INTRA - 2)).start()

    for copy in w_copies:
        copy.wait()

    proj_f[...] = proj[...].astype(F32)
    weight = jnp.concatenate([proj_f[pl.ds(q, N_TOWER, stride=QV), :] for q in range(QV)], axis=0)
    proj[...] = weight.astype(BF16)

    for c in range(NCH):
        steps = steps_of(c)
        rows = ROWS[c]
        arrived = recv[c].at[pl.ds(0, N_INTRA - 1)]
        pltpu.make_async_copy(arrived, arrived, recv_sem.at[c]).wait()
        for m in range(TOW_DEV):
            for s in range(TFEAT):
                x[m, 0:rows, s * EDIM : (s + 1) * EDIM] = recv[c][assign[0, m * TFEAT + s]]
        result = []
        for m in range(TOW_DEV):
            for n in range(HID // 256):
                cols = slice(n * 256, (n + 1) * 256)
                total = jnp.dot(x[m, 0:rows, :], w1[m, :, cols], preferred_element_type=F32)
                hid[m, 0:rows, cols] = jnp.maximum(total + b1[pl.ds(m, 1), cols], 0.0).astype(BF16)
            total = jnp.dot(hid[m, 0:rows, :], w2[m], preferred_element_type=F32)
            result.append(jnp.maximum(total + b2[pl.ds(m, 1), :], 0.0))
        copies = []
        for pos, (dx, dy) in enumerate(steps):
            block = jnp.concatenate(
                [
                    result[q // 2][pos * SD : (pos + 1) * SD, (q % 2) * EDIM : (q % 2 + 1) * EDIM]
                    for q in range(QV)
                ],
                axis=0,
            ).astype(BF16)
            if (dx, dy) == (0, 0):
                own[tower] = block
                continue
            slot = FIRST[c] + pos
            send[slot] = block
            copies.append(
                pltpu.make_async_remote_copy(
                    src_ref=send.at[slot],
                    dst_ref=own.at[tower],
                    send_sem=send2_sem,
                    recv_sem=recv2_sem,
                    device_id=place(*target_of(dx, dy), z, core),
                    device_id_type=MESH,
                )
            )
        for pos, (dx, dy) in enumerate(steps):
            if dx == 0 and pos % RUN == 0:
                continue
            gx, gy = target_of(dx, dy)

            @pl.when(gy * 8 + gx > rank)
            def _(dx=dx, pos=pos):
                pl.semaphore_wait(ready2.at[dx * RUN + pos % RUN], 1)

        for copy in copies:
            copy.start()

    arrived = own.at[pl.ds(0, N_TOWER - 1)]
    pltpu.make_async_copy(arrived, arrived, recv2_sem).wait()

    own_f[...] = own[...].astype(F32).reshape(N_TOWER * QV * SD, EDIM)
    weight = proj[...]
    for r in range(SD):
        vectors = jnp.concatenate(
            [own_f[pl.ds(q * SD + r, N_TOWER, stride=QV * SD), :] for q in range(QV)], axis=0
        ).astype(BF16)
        gram = lax.dot_general(
            vectors, vectors, (((1,), (1,)), ((), ())), preferred_element_type=F32
        ) * (1.0 / EDIM)
        high = gram.astype(BF16)
        low = (gram - high.astype(F32)).astype(BF16)
        result = jnp.dot(high, weight, preferred_element_type=F32)
        result = result + jnp.dot(low, weight, preferred_element_type=F32)
        for q in range(QV):
            out_f[r, pl.ds(q, N_TOWER, stride=QV), :] = result[q * N_TOWER : (q + 1) * N_TOWER, :]
        out[r] = out_f[r].astype(BF16)

    for c in range(NCH):
        left = stage[c].at[pl.ds(0, N_INTRA - 1)]
        pltpu.make_async_copy(left, left, send_sem.at[c]).wait()
    left = own.at[pl.ds(0, N_TOWER - 1)]
    pltpu.make_async_copy(left, left, send2_sem).wait()


def shards(
    embeddings,
    feature_assign,
    sample_owner,
    first_weight,
    first_bias,
    tower_weight,
    tower_bias,
    proj_weight,
):
    vmem = pl.BlockSpec(memory_space=pltpu.VMEM)
    hbm = pl.BlockSpec(memory_space=pltpu.HBM)
    dma = pltpu.SemaphoreType.DMA
    blocks = [pltpu.VMEM((N_INTRA, rows, EDIM), BF16) for rows in ROWS]
    return pl.pallas_call(
        kernel,
        out_shape=jax.ShapeDtypeStruct((SD, N_TOWER * QV, EDIM), BF16),
        in_specs=[hbm] * 8,
        out_specs=vmem,
        scratch_shapes=[
            *blocks,
            *blocks,
            pltpu.SMEM((SAMPLES,), jnp.int32),
            pltpu.SMEM((1, TOW_DEV * TFEAT), jnp.int32),
            pltpu.VMEM((TOW_DEV, HID), F32),
            pltpu.VMEM((TOW_DEV, TOUT), F32),
            pltpu.VMEM((N_TOWER * QV, EDIM), BF16),
            pltpu.VMEM((SAMPLES, EDIM), BF16),
            pltpu.VMEM((SAMPLES, EDIM), F32),
            pltpu.VMEM((TOW_DEV, TIN, HID), BF16),
            pltpu.VMEM((TOW_DEV, HID, TOUT), BF16),
            pltpu.VMEM((max(ROWS), EDIM), F32),
            pltpu.VMEM((TOW_DEV, max(ROWS), TIN), BF16),
            pltpu.VMEM((TOW_DEV, max(ROWS), HID), BF16),
            pltpu.VMEM((N_TOWER, QV * SD, EDIM), BF16),
            pltpu.VMEM((N_TOWER, QV * SD, EDIM), BF16),
            pltpu.VMEM((N_TOWER * QV * SD, EDIM), F32),
            pltpu.VMEM((SD, N_TOWER * QV, EDIM), F32),
            pltpu.VMEM((N_TOWER * QV, EDIM), F32),
            dma((EMB_PARTS,)),
            dma,
            dma((6,)),
            dma((NCH,)),
            dma((NCH,)),
            dma,
            dma,
            pltpu.SemaphoreType.REGULAR((N_INTRA,)),
            pltpu.SemaphoreType.REGULAR((N_TOWER,)),
        ],
        compiler_params=pltpu.CompilerParams(
            collective_id=0, has_side_effects=True, vmem_limit_bytes=67043328
        ),
        name="towers",
    )(
        sample_owner,
        feature_assign,
        embeddings,
        first_weight,
        first_bias,
        tower_weight,
        tower_bias,
        proj_weight,
    )


def solution(mesh):
    return jax.shard_map(
        shards,
        mesh=mesh,
        in_specs=(
            P(None, ("tower", "intra")),
            P("tower", None),
            P(),
            P("tower", None, None),
            P("tower", None),
            P("tower", None, None),
            P("tower", None),
            P(),
        ),
        out_specs=P(("tower", "intra"), None, None),
        check_vma=False,
    )
```

```python
import jax
import jax.numpy as jnp
from jax import lax
from jax.experimental import pallas as pl
from jax.experimental.pallas import tpu as pltpu
from jax.sharding import PartitionSpec as P

EDIM = 128
TOW_DEV = 2
TFEAT = 16
TIN = 2048
HID = 1024
TOUT = 256
SD = 8
QV = 4
N_TOWER = 32
N_INTRA = 32
SAMPLES = 8192
CHUNKS = ((4, 5), (3, 6), (2, 7), (1,), (0,))
NCH = len(CHUNKS)
RUN = 4
ROWS = tuple(len(offsets) * RUN * SD for offsets in CHUNKS)
FIRST = tuple(RUN * sum(len(offsets) for offsets in CHUNKS[:c]) for c in range(NCH))
EMB_PARTS = 4
MESH = pl.DeviceIdType.MESH
BF16 = jnp.bfloat16
F32 = jnp.float32


def kernel(
    owner_hbm, assign_hbm, emb_hbm, w1_hbm, b1_hbm, w2_hbm, b2_hbm, proj_hbm, out, *scratch
):
    stage, recv = scratch[:NCH], scratch[NCH : 2 * NCH]
    (
        owner, assign, b1, b2, proj, emb_b, emb_f, w1, w2, rows_f, x, hid, send, own, own_f, out_f, proj_f,
        emb_sem, table_sem, w_sem, send_sem, recv_sem, send2_sem, recv2_sem, ready, ready2,
    ) = scratch[2 * NCH :]
    tower = lax.axis_index("tower")
    me = lax.axis_index("intra")
    tx = tower // RUN
    y = (me // 16) * RUN + tower % RUN
    z, core = (me // 2) % 8, me % 2

    part = SAMPLES // EMB_PARTS
    emb_copies = [
        pltpu.make_async_copy(
            emb_hbm.at[pl.ds(i * part, part)], emb_b.at[pl.ds(i * part, part)], emb_sem.at[i]
        )
        for i in range(EMB_PARTS)
    ]
    owner_copy = pltpu.make_async_copy(owner_hbm, owner, table_sem)
    others = ((assign_hbm, assign), (b1_hbm, b1), (b2_hbm, b2), (proj_hbm, proj), (w2_hbm, w2), (w1_hbm, w1))
    w_copies = [
        pltpu.make_async_copy(source, target, w_sem.at[i]) for i, (source, target) in enumerate(others)
    ]
    owner_copy.start()
    for copy in emb_copies:
        copy.start()

    barrier = pltpu.get_barrier_semaphore()

    def place(px, py, pz, pcore):
        return {"tower": px * RUN + py % RUN, "intra": (py // RUN) * 16 + pz * 2 + pcore}

    def y_step(dx, step):
        return (step % 2) * (2 - step) + (step // 2) * (1 - step % 2) * (2 - 4 * (dx % 2))

    def member(order):
        return tx, (y % RUN) + RUN * ((order // 2) % 2), order // 4, order % 2

    def source_of(k):
        dx = k // RUN
        return (tx + 8 - dx) % 8, (y + 8 - y_step(dx, k % RUN)) % 8

    def target_of(dx, dy):
        return (tx + dx) % 8, (y + 8 + dy) % 8

    order = z * 4 + (y // RUN) * 2 + core
    rank = y * 8 + tx

    @pl.loop(order + 1, N_INTRA)
    def _(later):
        pl.semaphore_signal(barrier, inc=1, device_id=place(*member(later)), device_id_type=MESH)

    def greet(k, count):
        sx, sy = source_of(k)
        gx, gy = target_of(k // RUN, y_step(k // RUN, k % RUN))

        @pl.when(sy * 8 + sx > rank)
        def _():
            pl.semaphore_signal(barrier, inc=1, device_id=place(sx, sy, z, core), device_id_type=MESH)

        @pl.when(gy * 8 + gx > rank)
        def _():
            pl.semaphore_signal(barrier, inc=1, device_id=place(gx, gy, z, core), device_id_type=MESH)

        count = count + jnp.where(sy * 8 + sx < rank, 1, 0)
        return count + jnp.where(gy * 8 + gx < rank, 1, 0)

    earlier = lax.fori_loop(1, N_TOWER, greet, order)

    for i, copy in enumerate(emb_copies):
        copy.wait()
        emb_f[pl.ds(i * part, part), :] = emb_b[pl.ds(i * part, part), :].astype(F32)
    for copy in w_copies:
        copy.start()
    owner_copy.wait()

    def steps_of(c):
        return [(dx, y_step(dx, step)) for dx in CHUNKS[c] for step in range(RUN)]

    def peer_of(k):
        kk = 7 - k % 8
        odd = kk % 2
        dz = odd * ((kk + 1) // 2) + (1 - odd) * (8 - kk // 2)
        dy = 1 - (k // 8) % 2
        dc = 1 - k // 16
        return tx, (y + RUN * dy) % 8, (z + dz) % 8, (core + dc) % 2

    def gather(steps, peer):
        rows = len(steps) * SD
        px, py, pz, pcore = peer
        for pos, (dx, dy) in enumerate(steps):
            target = place((px + dx) % 8, (py + 8 + dy) % 8, pz, pcore)
            base = (target["tower"] * N_INTRA + target["intra"]) * SD
            for r in range(SD):
                rows_f[pl.ds(pos * SD + r, 1), :] = emb_f[pl.ds(owner[base + r], 1), :]
        return rows_f[pl.ds(0, rows), :].astype(BF16)

    @pl.when(earlier > 0)
    def _():
        pl.semaphore_wait(barrier, earlier)

    @pl.loop(0, order)
    def _(sooner):
        pl.semaphore_signal(ready.at[me], inc=1, device_id=place(*member(sooner)), device_id_type=MESH)

    @pl.loop(1, N_TOWER)
    def _(k):
        sx, sy = source_of(k)

        @pl.when(sy * 8 + sx < rank)
        def _():
            pl.semaphore_signal(
                ready2.at[k], inc=1, device_id=place(sx, sy, z, core), device_id_type=MESH
            )

    def copy_of(c, slot, peer):
        return pltpu.make_async_remote_copy(
            src_ref=stage[c].at[slot],
            dst_ref=recv[c].at[me],
            send_sem=send_sem.at[c],
            recv_sem=recv_sem.at[c],
            device_id=place(*peer),
            device_id_type=MESH,
        )

    def order_of(peer):
        return peer[2] * 4 + (peer[1] // RUN) * 2 + peer[3]

    def send_first(at):
        copy_of(0, at, member(at)).start()

    def first(k, before):
        peer = peer_of(k)
        at = order_of(peer)
        stage[0][at] = gather(steps_of(0), peer)

        @pl.when(before < order)
        def _():
            send_first(before)

        return at

    last = lax.fori_loop(0, N_INTRA - 1, first, order)
    recv[0][me] = gather(steps_of(0), (tx, y, z, core))

    @pl.when(last < order)
    def _():
        send_first(last)

    @pl.loop(order + 1, N_INTRA)
    def _(at):
        pl.semaphore_wait(ready.at[place(*member(at))["intra"]], 1)
        send_first(at)

    for c in range(1, NCH):
        steps = steps_of(c)

        @pl.loop(0, N_INTRA - 1)
        def _(k, c=c, steps=steps):
            stage[c][k] = gather(steps, peer_of(k))

            @pl.when(k > 0)
            def _():
                copy_of(c, k - 1, peer_of(k - 1)).start()

        recv[c][me] = gather(steps, (tx, y, z, core))
        copy_of(c, N_INTRA - 2, peer_of(N_INTRA - 2)).start()

    for copy in w_copies:
        copy.wait()

    proj_f[...] = proj[...].astype(F32)
    weight = jnp.concatenate([proj_f[pl.ds(q, N_TOWER, stride=QV), :] for q in range(QV)], axis=0)
    proj[...] = weight.astype(BF16)

    for c in range(NCH):
        steps = steps_of(c)
        rows = ROWS[c]
        arrived = recv[c].at[pl.ds(0, N_INTRA - 1)]
        pltpu.make_async_copy(arrived, arrived, recv_sem.at[c]).wait()
        for m in range(TOW_DEV):
            for s in range(TFEAT):
                x[m, 0:rows, s * EDIM : (s + 1) * EDIM] = recv[c][assign[0, m * TFEAT + s]]
        result = []
        for m in range(TOW_DEV):
            for n in range(HID // 256):
                cols = slice(n * 256, (n + 1) * 256)
                total = jnp.dot(x[m, 0:rows, :], w1[m, :, cols], preferred_element_type=F32)
                hid[m, 0:rows, cols] = jnp.maximum(total + b1[pl.ds(m, 1), cols], 0.0).astype(BF16)
            total = jnp.dot(hid[m, 0:rows, :], w2[m], preferred_element_type=F32)
            result.append(jnp.maximum(total + b2[pl.ds(m, 1), :], 0.0))
        copies = []
        for pos, (dx, dy) in enumerate(steps):
            block = jnp.concatenate(
                [
                    result[q // 2][pos * SD : (pos + 1) * SD, (q % 2) * EDIM : (q % 2 + 1) * EDIM]
                    for q in range(QV)
                ],
                axis=0,
            ).astype(BF16)
            if (dx, dy) == (0, 0):
                own[tower] = block
                continue
            slot = FIRST[c] + pos
            send[slot] = block
            copies.append(
                pltpu.make_async_remote_copy(
                    src_ref=send.at[slot],
                    dst_ref=own.at[tower],
                    send_sem=send2_sem,
                    recv_sem=recv2_sem,
                    device_id=place(*target_of(dx, dy), z, core),
                    device_id_type=MESH,
                )
            )
        for pos, (dx, dy) in enumerate(steps):
            if dx == 0 and pos % RUN == 0:
                continue
            gx, gy = target_of(dx, dy)

            @pl.when(gy * 8 + gx > rank)
            def _(dx=dx, pos=pos):
                pl.semaphore_wait(ready2.at[dx * RUN + pos % RUN], 1)

        for copy in copies:
            copy.start()

    arrived = own.at[pl.ds(0, N_TOWER - 1)]
    pltpu.make_async_copy(arrived, arrived, recv2_sem).wait()

    own_f[...] = own[...].astype(F32).reshape(N_TOWER * QV * SD, EDIM)
    weight = proj[...]
    for r in range(SD):
        vectors = jnp.concatenate(
            [own_f[pl.ds(q * SD + r, N_TOWER, stride=QV * SD), :] for q in range(QV)], axis=0
        ).astype(BF16)
        gram = lax.dot_general(
            vectors, vectors, (((1,), (1,)), ((), ())), preferred_element_type=F32
        ) * (1.0 / EDIM)
        high = gram.astype(BF16)
        low = (gram - high.astype(F32)).astype(BF16)
        result = jnp.dot(high, weight, preferred_element_type=F32)
        result = result + jnp.dot(low, weight, preferred_element_type=F32)
        for q in range(QV):
            out_f[r, pl.ds(q, N_TOWER, stride=QV), :] = result[q * N_TOWER : (q + 1) * N_TOWER, :]
        out[r] = out_f[r].astype(BF16)

    for c in range(NCH):
        left = stage[c].at[pl.ds(0, N_INTRA - 1)]
        pltpu.make_async_copy(left, left, send_sem.at[c]).wait()
    left = own.at[pl.ds(0, N_TOWER - 1)]
    pltpu.make_async_copy(left, left, send2_sem).wait()


def shards(
    embeddings,
    feature_assign,
    sample_owner,
    first_weight,
    first_bias,
    tower_weight,
    tower_bias,
    proj_weight,
):
    vmem = pl.BlockSpec(memory_space=pltpu.VMEM)
    hbm = pl.BlockSpec(memory_space=pltpu.HBM)
    dma = pltpu.SemaphoreType.DMA
    blocks = [pltpu.VMEM((N_INTRA, rows, EDIM), BF16) for rows in ROWS]
    return pl.pallas_call(
        kernel,
        out_shape=jax.ShapeDtypeStruct((SD, N_TOWER * QV, EDIM), BF16),
        in_specs=[hbm] * 8,
        out_specs=vmem,
        scratch_shapes=[
            *blocks,
            *blocks,
            pltpu.SMEM((SAMPLES,), jnp.int32),
            pltpu.SMEM((1, TOW_DEV * TFEAT), jnp.int32),
            pltpu.VMEM((TOW_DEV, HID), F32),
            pltpu.VMEM((TOW_DEV, TOUT), F32),
            pltpu.VMEM((N_TOWER * QV, EDIM), BF16),
            pltpu.VMEM((SAMPLES, EDIM), BF16),
            pltpu.VMEM((SAMPLES, EDIM), F32),
            pltpu.VMEM((TOW_DEV, TIN, HID), BF16),
            pltpu.VMEM((TOW_DEV, HID, TOUT), BF16),
            pltpu.VMEM((max(ROWS), EDIM), F32),
            pltpu.VMEM((TOW_DEV, max(ROWS), TIN), BF16),
            pltpu.VMEM((TOW_DEV, max(ROWS), HID), BF16),
            pltpu.VMEM((N_TOWER, QV * SD, EDIM), BF16),
            pltpu.VMEM((N_TOWER, QV * SD, EDIM), BF16),
            pltpu.VMEM((N_TOWER * QV * SD, EDIM), F32),
            pltpu.VMEM((SD, N_TOWER * QV, EDIM), F32),
            pltpu.VMEM((N_TOWER * QV, EDIM), F32),
            dma((EMB_PARTS,)),
            dma,
            dma((6,)),
            dma((NCH,)),
            dma((NCH,)),
            dma,
            dma,
            pltpu.SemaphoreType.REGULAR((N_INTRA,)),
            pltpu.SemaphoreType.REGULAR((N_TOWER,)),
        ],
        compiler_params=pltpu.CompilerParams(
            collective_id=0, has_side_effects=True, vmem_limit_bytes=67043328
        ),
        name="towers",
    )(
        sample_owner,
        feature_assign,
        embeddings,
        first_weight,
        first_bias,
        tower_weight,
        tower_bias,
        proj_weight,
    )


def solution(mesh):
    return jax.shard_map(
        shards,
        mesh=mesh,
        in_specs=(
            P(None, ("tower", "intra")),
            P("tower", None),
            P(),
            P("tower", None, None),
            P("tower", None),
            P("tower", None, None),
            P("tower", None),
            P(),
        ),
        out_specs=P(("tower", "intra"), None, None),
        check_vma=False,
    )
```
